512 devices in a mesh: seq: 64 (over y, x, core), expert: 8 (over z).
Axes of the slice: x: 4, y: 8, z: 8, core: 2. Of those that a mesh axis runs over, the one named last changes fastest.
Arguments:
- query_cols: bfloat16 [256, 131072], P('expert', 'seq'), may hold values from -16 to 16
- key_cols: bfloat16 [256, 131072], P('expert', 'seq'), may hold values from -6 to 6
- value_cols: bfloat16 [256, 131072], P('expert', 'seq'), may hold values from -12 to 12
- block_list: int32 [1024, 4], P('seq'), may hold values from 0 to 1023, as said below
- residual: bfloat16 [131072, 256], P(('seq', 'expert')), may hold values from -6 to 6
- out_proj: bfloat16 [256, 256], replicated, may hold values from -0.375 to 0.375
- norm_gain: float32 [256], replicated, may hold values from 0.1 to 1.9
- router_weight: bfloat16 [256, 16], replicated, may hold values from -0.375 to 0.375
- expert_ids: int32 [131072, 2], P(('seq', 'expert')), may hold values from 0 to 15, all different within a row; in each aligned block of 256 rows (0 to 255, 256 to 511, ...) at most 64 rows name the same one
- expert_in: bfloat16 [16, 256, 512], P('expert'), may hold values from -0.375 to 0.375
- expert_out: bfloat16 [16, 512, 256], P('expert'), may hold values from -0.25 to 0.25
- cotangent: bfloat16 [131072, 256], P(('seq', 'expert')), may hold values from -6 to 6
Outputs:
- layer_out: bfloat16 [131072, 256], P(('seq', 'expert'))
- grad_stream: bfloat16 [131072, 256], P(('seq', 'expert'))
- grad_w_in: float32 [16, 256, 512], P('expert')
- grad_w_out: float32 [16, 512, 256], P('expert')
The draws below stay inside these ranges and needn't reach their ends.
Inputs may be any that keep to these rules, and one draw needn't show every extreme that they name: `block_list`: global key block ids. Among the entries of the 16 query blocks of one seq index, no owner index (id // 16) appears more than 2 times, and one owner, the same for every seq index, appears exactly 2 times. A row may repeat a block. `expert_ids`: each row names 2 different experts; in each aligned block of 256 rows (the rows of one device) no expert is named more than 64 times.
All inputs are finite; a program needn't handle non-finite values.
Results may differ from the reference program's by a relative error of at most 0.0081.
Values may be sent and summed in bfloat16 or wider, within the bound.
A program may use at most 64 MiB of HBM per device.

```python
import math
import jax
import jax.numpy as jnp
import numpy as np
from jax import lax

D = 256
HEADS = 8
HD = 32
FF = 512
EXPERTS = 16
TOPK = 2
BLOCK = 128
DEG = 4
BLK_SEQ = 16
NBLK = 1024
NODES = 131072
T_DEV = 256
CAP = 2
CAPE = 64


def block_table(key):
    device_count = NBLK // BLK_SEQ
    pair_count = BLK_SEQ * DEG
    slot_count = device_count * CAP
    hot_owner = jax.random.randint(jax.random.fold_in(key, 7), (), 0, device_count)
    slot_owner = jnp.arange(slot_count, dtype=jnp.int32) // CAP
    slot_range = jnp.arange(slot_count, dtype=jnp.int32)

    def one_device(device_index):
        device_key = jax.random.fold_in(key, 100 + device_index)
        ranking = jax.random.permutation(jax.random.fold_in(device_key, 1), slot_count).astype(jnp.int32)
        score_ints = jnp.where(slot_owner == hot_owner, slot_range - slot_count, ranking)
        picked = jnp.argsort(score_ints, stable=True)[:pair_count]
        owners = slot_owner[picked]
        shuffle = jax.random.permutation(jax.random.fold_in(device_key, 2), pair_count)
        owners = owners[shuffle]
        inner_ids = jax.random.randint(jax.random.fold_in(device_key, 3), (pair_count,), 0, BLK_SEQ)
        return (owners * BLK_SEQ + inner_ids).astype(jnp.int32)
    table = jax.vmap(one_device)(jnp.arange(device_count, dtype=jnp.int32))
    return table.reshape(NBLK, DEG)


def drawn_keys(key):
    base_key = jax.random.fold_in(key, 21)
    return jax.random.truncated_normal(jax.random.fold_in(base_key, 1), -6.0, 6.0, (D, NODES), jnp.float32)


def draw_block_list(key, part):
    return block_table(jax.random.fold_in(key, 11))


def draw_key_cols(key, part):
    field = drawn_keys(key)
    return field.astype(jnp.bfloat16)


def draw_query_cols(key, part):
    base_key = jax.random.fold_in(key, 31)
    field = 1.5 * jax.random.truncated_normal(jax.random.fold_in(base_key, 1), -6.0, 6.0, (D, NODES), jnp.float32)
    return field.astype(jnp.bfloat16)


def levels(rng, shape, shards, least, largest):
    loudness, own = 1.0, jax.random.fold_in(rng, 6)
    for dim, blocks in shards:
        steps = jnp.exp(jax.random.uniform(jax.random.fold_in(own, dim), (blocks,), jnp.float32, least / len(shards), largest / len(shards)))
        loudness = loudness * jnp.repeat(steps, shape[dim] // blocks).reshape([-1 if axis == dim else 1 for axis in range(len(shape))])
    return loudness


def assign_block(own_key, own, number, rows, amount, top, most, slope):
    sequence = jax.random.permutation(own_key, amount)
    crowded, ordinary = portions_of(amount, rows * top, most, slope, True), portions_of(amount, rows * top, most, slope, False)
    places = jnp.arange(amount)

    def named(tallies, rotation):
        used = int((tallies > 0).sum())
        fixed = max(1, used // 4)
        shifted = fixed + (places - fixed + rotation * (used - fixed)) % max(1, amount - fixed)
        return jnp.zeros((amount,), jnp.int32).at[sequence[jnp.where(places < fixed, places, shifted)]].set(jnp.asarray(tallies, jnp.int32))

    tallies = jnp.where(number % 4 == 0, named(crowded, number // 4), named(ordinary, number - number // 4 - 1))
    mixed = jax.random.permutation(jax.random.fold_in(own, 3), amount)
    donor, sink = mixed[0:amount // 2 * 2:2], mixed[1:amount // 2 * 2:2]
    room = jnp.minimum(tallies[donor] - 1, most - tallies[sink]) // 2
    room = jnp.where((donor == sequence[0]) | (sink == sequence[0]) | (tallies[sink] == 0), 0, jnp.maximum(room, 0))
    shifted = jax.random.randint(jax.random.fold_in(own, 4), (amount // 2,), 0, 1 << 20) % (room + 1)
    tallies = tallies.at[donor].add(-shifted).at[sink].add(shifted)
    members = jnp.searchsorted(jnp.cumsum(tallies), jnp.arange(rows * top), side="right").astype(jnp.int32)
    table = members.reshape(top, rows).T
    table = table[jax.random.permutation(jax.random.fold_in(own, 1), rows)]
    rotation = jax.random.randint(jax.random.fold_in(own, 2), (rows, 1), 0, top)
    return jnp.take_along_axis(table, (jnp.arange(top)[None, :] + rotation) % top, axis=1)


def portions_of(amount, total, bound, slope, full):
    weights = [(1 << 20) // math.isqrt(rank ** slope) + 1 for rank in range(1, amount + 1)]
    largest = bound if full else min(bound, max(-(-total // amount), total * weights[0] // sum(weights)))
    least = 1 if total - largest >= amount - 1 else 0
    holding, spare = [largest] + [least] * (amount - 1), total - largest - least * (amount - 1)
    while spare > 0:
        movable = [i for i in range(1, amount) if holding[i] < largest] or [i for i in range(1, amount) if holding[i] < bound]
        pool, left = sum([weights[i] for i in movable]), spare
        for i in movable:
            more = min(bound - holding[i], max(1, left * weights[i] // pool), spare)
            holding[i] = holding[i] + more
            spare = spare - more
    return np.array(holding)


def noise(stream_key, shape, spread, most, split=(), held_as=jnp.bfloat16):
    result = spread * jax.random.normal(stream_key, shape, jnp.float32)
    if split:
        result = result * levels(stream_key, shape, split, -0.22, 0.18)
    return jnp.clip(result, -most, most).astype(held_as)


def setup_inputs(seed: int = 0) -> dict:
    key_of = jax.random.split(jax.random.key(seed), 13)
    query_cols = draw_query_cols(jax.random.fold_in(key_of[12], 71), 0)
    key_cols = draw_key_cols(jax.random.fold_in(key_of[12], 71), 0)
    value_cols = noise(key_of[2], (D, NODES), 2.0, 12.0, ((0, 8), (1, 64)))
    block_list = draw_block_list(jax.random.fold_in(key_of[12], 71), 0)
    residual = noise(key_of[4], (NODES, D), 1.0, 6.0, ((0, 512),))
    out_proj = noise(key_of[5], (D, D), D ** -0.5, 0.375)
    norm_gain = jnp.clip(1.0 + 0.18 * jax.random.normal(key_of[6], (D,), jnp.float32), 0.1, 1.9)
    router_weight = noise(key_of[7], (D, EXPERTS), D ** -0.5, 0.375)
    expert_ids_keys = jax.random.split(jax.random.fold_in(key_of[8], 1), NODES // T_DEV)
    expert_ids_turns = jax.random.permutation(jax.random.fold_in(key_of[8], 3), NODES // T_DEV)
    expert_ids = jax.vmap(lambda own, number: assign_block(jax.random.fold_in(key_of[8], 2), own, number, T_DEV, EXPERTS, TOPK, CAPE, 2))(expert_ids_keys, expert_ids_turns).reshape((NODES, TOPK))
    expert_in = noise(key_of[9], (EXPERTS, D, FF), D ** -0.5, 0.375, ((0, 8),))
    expert_out = noise(key_of[10], (EXPERTS, FF, D), FF ** -0.5, 0.25, ((0, 8),))
    cotangent = noise(key_of[11], (NODES, D), 1.0, 6.0, ((0, 512),))
    return dict(query_cols=query_cols, key_cols=key_cols, value_cols=value_cols, block_list=block_list, residual=residual, out_proj=out_proj, norm_gain=norm_gain, router_weight=router_weight, expert_ids=expert_ids, expert_in=expert_in, expert_out=expert_out, cotangent=cotangent)


norm_eps = 1e-05
root_two_pi = 0.7978845608028654
cubic_term = 0.044715

def gelu_value(preact):
    inside = root_two_pi * (preact + cubic_term * preact * preact * preact)
    return 0.5 * preact * (1.0 + jnp.tanh(inside))

def gelu_slope(preact):
    inside = root_two_pi * (preact + cubic_term * preact * preact * preact)
    tanh_value = jnp.tanh(inside)
    return 0.5 * (1.0 + tanh_value) + 0.5 * preact * (1.0 - tanh_value * tanh_value) * root_two_pi * (1.0 + 3.0 * cubic_term * preact * preact)

def as_wide(values):
    return lax.optimization_barrier(values).astype(jnp.float32)

def attend_all(query_cols, key_cols, value_cols, block_list):
    query_blocks = query_cols.reshape(HEADS, HD, NBLK, BLOCK)
    key_blocks = key_cols.reshape(HEADS, HD, NBLK, BLOCK)
    value_blocks = value_cols.reshape(HEADS, HD, NBLK, BLOCK)
    scale_factor = 1.0 / math.sqrt(HD)
    highest = lax.Precision.HIGHEST

    def one_block(inputs):
        block_index, listed = inputs
        queries = lax.dynamic_index_in_dim(query_blocks, block_index, 2, keepdims=False).astype(jnp.float32)
        keys = jnp.take(key_blocks, listed, axis=2).reshape(HEADS, HD, DEG * BLOCK).astype(jnp.float32)
        values = jnp.take(value_blocks, listed, axis=2).reshape(HEADS, HD, DEG * BLOCK).astype(jnp.float32)
        scores = jnp.einsum('hdn,hdj->hnj', queries, keys, precision=highest) * scale_factor
        row_max = lax.optimization_barrier(jnp.max(scores, -1, keepdims=True))
        weights = jnp.exp(scores - row_max)
        row_sum = lax.optimization_barrier(jnp.sum(weights, -1))
        rounded = as_wide(weights.astype(jnp.bfloat16))
        attended = jnp.einsum('hnj,hdj->hdn', rounded, values, precision=highest) / row_sum[:, None, :]
        return attended.astype(jnp.bfloat16)
    outputs = lax.map(one_block, (jnp.arange(NBLK, dtype=jnp.int32), block_list))
    return jnp.transpose(outputs, (1, 2, 0, 3)).reshape(HEADS * HD, NODES)

def reference(query_cols, key_cols, value_cols, block_list, residual, out_proj, norm_gain, router_weight, expert_ids, expert_in, expert_out, cotangent):
    highest = lax.Precision.HIGHEST
    attended = attend_all(query_cols, key_cols, value_cols, block_list)
    projected = jnp.dot(attended.T, out_proj, preferred_element_type=jnp.float32)
    stream = (residual.astype(jnp.float32) + projected).astype(jnp.bfloat16)
    block_count = NODES // T_DEV
    full_in = expert_in.astype(jnp.float32)
    full_out = expert_out.astype(jnp.float32)
    router_float = router_weight.astype(jnp.float32)
    expert_range = jnp.arange(EXPERTS, dtype=jnp.int32)

    def step(carry, inputs):
        stream_rows, id_rows, cot_rows = inputs
        stream_float = stream_rows.astype(jnp.float32)
        inverse_rms = lax.rsqrt(lax.optimization_barrier(jnp.mean(stream_float * stream_float, -1, keepdims=True)) + norm_eps)
        normed = (stream_float * inverse_rms * norm_gain).astype(jnp.bfloat16)
        logits = jnp.dot(normed, router_weight, preferred_element_type=jnp.float32)
        gate_values = jax.nn.sigmoid(jnp.take_along_axis(logits, id_rows, 1))
        flat_ids = id_rows.reshape(-1)
        flat_hot = (flat_ids[:, None] == expert_range[None, :]).astype(jnp.int32)
        slot_rank = lax.optimization_barrier(jnp.sum((jnp.cumsum(flat_hot, 0) - flat_hot) * flat_hot, 1))
        position = flat_ids * CAPE + slot_rank

        def pack_rows(rows):
            filled = jnp.zeros((EXPERTS * CAPE, D), jnp.bfloat16).at[position].set(rows)
            return filled.reshape(EXPERTS, CAPE, D)

        def unpack_rows(buffer):
            return jnp.take(buffer.reshape(EXPERTS * CAPE, D), position, axis=0).reshape(T_DEV, TOPK, D)
        rows_in = as_wide(pack_rows(jnp.repeat(normed, TOPK, 0)))
        preact = jnp.einsum('erd,edf->erf', rows_in, full_in, precision=highest)
        hidden = gelu_value(preact).astype(jnp.bfloat16)
        hidden_wide = as_wide(hidden)
        produced = jnp.einsum('erf,efd->erd', hidden_wide, full_out, precision=highest).astype(jnp.bfloat16)
        expert_rows = as_wide(unpack_rows(produced))
        cot_float = cot_rows.astype(jnp.float32)
        layer_rows = (stream_float + lax.optimization_barrier(jnp.sum(gate_values[:, :, None] * expert_rows, 1))).astype(jnp.bfloat16)
        scaled = (gate_values[:, :, None] * cot_float[:, None, :]).astype(jnp.bfloat16).reshape(T_DEV * TOPK, D)
        cot_buffer = as_wide(pack_rows(scaled))
        grad_out = jnp.einsum('erf,erd->efd', hidden_wide, cot_buffer, precision=highest)
        grad_hidden = jnp.einsum('erd,efd->erf', cot_buffer, full_out, precision=highest)
        grad_pre = as_wide((grad_hidden * gelu_slope(preact)).astype(jnp.bfloat16))
        grad_in = jnp.einsum('erd,erf->edf', rows_in, grad_pre, precision=highest)
        grad_back = jnp.einsum('erf,edf->erd', grad_pre, full_in, precision=highest).astype(jnp.bfloat16)
        grad_gate = lax.optimization_barrier(jnp.sum(cot_float[:, None, :] * expert_rows, -1))
        grad_logit = grad_gate * gate_values * (1.0 - gate_values)
        id_hot = id_rows[:, :, None] == expert_range[None, None, :]
        logit_table = lax.optimization_barrier(jnp.sum(jnp.where(id_hot, grad_logit[:, :, None], 0.0), 1))
        router_term = jnp.dot(logit_table, router_float.T, precision=highest)
        grad_normed = lax.optimization_barrier(jnp.sum(as_wide(unpack_rows(grad_back)), 1)) + router_term
        gained = grad_normed * norm_gain
        grad_rows = cot_float + inverse_rms * gained - stream_float * inverse_rms ** 3 * lax.optimization_barrier(jnp.mean(stream_float * gained, -1, keepdims=True))
        return ((carry[0] + grad_in, carry[1] + grad_out), (layer_rows, grad_rows.astype(jnp.bfloat16)))
    start = (jnp.zeros((EXPERTS, D, FF), jnp.float32), jnp.zeros((EXPERTS, FF, D), jnp.float32))
    inputs = (stream.reshape(block_count, T_DEV, D), expert_ids.reshape(block_count, T_DEV, TOPK), cotangent.reshape(block_count, T_DEV, D))
    (grad_w_in, grad_w_out), (layer_out, grad_stream) = lax.scan(step, start, inputs)
    return (layer_out.reshape(NODES, D), grad_stream.reshape(NODES, D), grad_w_in, grad_w_out)
```

```python
import math

import jax
import jax.numpy as jnp
from jax import lax
from jax.experimental import pallas as pl
from jax.experimental.pallas import tpu as pltpu
from jax.sharding import PartitionSpec as P

MESH = pl.DeviceIdType.MESH
BF = jnp.bfloat16
F32 = jnp.float32
HD = 32
NY, NX, NC, NZ = 8, 4, 2, 8
CAPE = 64

norm_eps = 1e-05
root_two_pi = 0.7978845608028654
cubic_term = 0.044715

TN = (((0,), (0,)), ((), ()))
NT = (((1,), (1,)), ((), ()))


def dot(a, b, dims=(((1,), (0,)), ((), ()))):
    return lax.dot_general(a, b, dims, preferred_element_type=F32)


def place():
    seq, z = lax.axis_index("seq"), lax.axis_index("expert")
    y = seq // (NX * NC)
    x = (seq // NC) % NX
    c = seq % NC
    return y, x, c, z


def device(y, x, c, z):
    return ((y * NX + x) * NC + c, z)


def send(src, dst, ssem, rsem, dev):
    copy = pltpu.make_async_remote_copy(
        src_ref=src, dst_ref=dst, send_sem=ssem, recv_sem=rsem, device_id=dev, device_id_type=MESH
    )
    copy.start()
    return copy


class Ring:
    def __init__(self, slots, ssem, rsem, up, down, far_up):
        self.slots, self.ssem, self.rsem = slots, ssem, rsem
        self.up, self.down, self.far_up = up, down, far_up
        self.copies = {}

    def go(self, frm, to, dev):
        self.copies[to] = send(self.slots(frm), self.slots(to), self.ssem(to), self.rsem(to), dev)

    def begin(self):
        self.go(0, 1, self.up)
        self.go(0, 7, self.down)

    def arrive(self, k):
        self.copies[k].wait_recv()
        if k < 3 or (k == 3 and self.far_up):
            self.go(k, k + 1, self.up)
        if k > 5 or (k == 5 and not self.far_up):
            self.go(k, k - 1, self.down)

    def finish(self):
        for copy in self.copies.values():
            copy.wait_send()


def exchange_kernel(
    idx, wtab, kv, q, res, cot, ids,
    att_all, res_all, cot_all, ids_all,
    yb1, yb2, yb3, yb4, yb5, yb6, yb7,
    zr, zc, zi, wr, wsm, sb, rv, at,
    y_s, y_r, z_s, z_r, w_s, w_r, x_s, x_r, a_s, a_r, l_s,
):
    y, x, c, z = place()
    up_y, down_y = device((y + 1) % NY, x, c, z), device((y + 7) % NY, x, c, z)
    up_z, down_z = device(y, x, c, (z + 1) % NZ), device(y, x, c, (z + 7) % NZ)
    row = [(dx, dc) for dx in range(NX) for dc in range(NC)]
    peers = [device(y, (x + dx) % NX, (c + dc) % NC, z) for dx, dc in row]

    barrier = pltpu.get_barrier_semaphore()
    for dev in [up_y, down_y, up_z, down_z] + peers[1:]:
        pl.semaphore_signal(barrier, inc=1, device_id=dev, device_id_type=MESH)
    pl.semaphore_wait(barrier, 11)

    ybs = [kv, yb1, yb2, yb3, yb4, yb5, yb6, yb7]
    tables = [
        send(wtab, wr.at[r], w_s.at[r], w_r.at[r], peers[r]) for r in range(1, 8)
    ]

    def y_ring(ch):
        return Ring(
            lambda k: ybs[k].at[pl.ds(ch * 8, 8)],
            lambda k: y_s.at[ch, k],
            lambda k: y_r.at[ch, k],
            up_y, down_y, ch == 0,
        )

    def z_ring(i, own, buf, far_up):
        return Ring(
            lambda k: own if k == 0 else buf.at[k],
            lambda k: z_s.at[i, k],
            lambda k: z_r.at[i, k],
            up_z, down_z, far_up,
        )

    ys = [y_ring(0), y_ring(1)]
    zs = [z_ring(0, res, zr, True), z_ring(1, cot, zc, False), z_ring(2, ids, zi, True)]
    zs[2].begin()
    for ch in range(2):
        ys[ch].begin()
        zs[ch].begin()

    own_table = pltpu.make_async_copy(wtab, wsm.at[0], l_s.at[0])
    own_table.start()
    for r in range(1, 8):
        tables[r - 1].wait_recv()
    rest = pltpu.make_async_copy(wr.at[pl.ds(1, 7)], wsm.at[pl.ds(1, 7)], l_s.at[1])
    rest.start()
    own_table.wait()
    rest.wait()

    line = x * NC + c
    moved = []

    def pick(rel):
        source = ybs[(8 - rel) % 8]
        owner_row = (y + rel) % NY
        for r, (dx, dc) in enumerate(row):
            asked = ((NX - dx) % NX) * NC + dc
            for s in range(2):
                block = wsm[asked, owner_row, line * 2 + s]
                if r == 0:
                    rv[rel * 2 + s] = source[block]
                else:
                    sb[rel, r, s] = source[block]
            if r:
                moved.append(
                    send(
                        sb.at[rel, r],
                        rv.at[pl.ds((r * 8 + rel) * 2, 2)],
                        x_s.at[r, rel],
                        x_r.at[r, rel],
                        peers[r],
                    )
                )

    pick(0)
    res_all[0] = res[...]
    cot_all[0] = cot[...]
    ids_all[0] = ids[...]
    for k in (1, 2, 3):
        for ch in range(2):
            for slot in (k, 8 - k):
                ys[ch].arrive(slot)
                zs[ch].arrive(slot)
        for slot in (k, 8 - k):
            zs[2].arrive(slot)
            pick((8 - slot) % 8)
            res_all[slot] = zr[slot]
            cot_all[slot] = zc[slot]
            ids_all[slot] = zi[slot]
    for ring in ys + zs:
        ring.arrive(4)
    pick(4)
    res_all[4] = zr[4]
    cot_all[4] = zc[4]
    ids_all[4] = zi[4]
    for copy in moved:
        copy.wait_recv()

    rings = []

    def attend(ch):
        def block(i, carry):
            b = ch * 4 + i
            pairs = [rv[idx[b * 4 + j]] for j in range(4)]
            keys = jnp.concatenate([p[:HD] for p in pairs], 1)
            values = jnp.concatenate([p[HD:] for p in pairs], 1)
            queries = q[:, pl.ds(pl.multiple_of(b * 128, 128), 128)]
            scores = dot(keys, queries, TN) * (1.0 / math.sqrt(HD))
            weights = jnp.exp(scores - jnp.max(scores, 0, keepdims=True))
            total = jnp.sum(weights, 0, keepdims=True)
            out = dot(values, weights.astype(BF)) / total
            at[0, ch, :, pl.ds(pl.multiple_of(i * 128, 128), 128)] = out.astype(BF)
            return carry

        lax.fori_loop(0, 4, block, 0)
        ring = Ring(
            lambda k: at.at[k, ch],
            lambda k: a_s.at[ch, k],
            lambda k: a_r.at[ch, k],
            up_z, down_z, ch < 2,
        )
        ring.begin()
        rings.append(ring)

    def keep(k, ch):
        head = (z + NZ - k) % NZ
        att_all[pl.ds(pl.multiple_of(head * HD, HD), HD), ch * 512 : (ch + 1) * 512] = at[k, ch]

    for ch in range(4):
        attend(ch)
    for ch in range(4):
        keep(0, ch)
    for k in (1, 2, 3):
        for ch in range(4):
            for slot in (k, 8 - k):
                rings[ch].arrive(slot)
        for ch in range(4):
            for slot in (k, 8 - k):
                keep(slot, ch)
    for ch in range(4):
        rings[ch].arrive(4)
        keep(4, ch)
    for ring in ys + zs + rings:
        ring.finish()
    for copy in tables + moved:
        copy.wait_send()


def expert_kernel(
    att, res, cot, ids, out_proj, gain, router, w_in, w_out,
    grads, layer_out, grad_stream,
    rows, cots, gates, ga, gb, ret, rr, hot_own, rank_own, stream_own, inv_own,
    rc, t1, rx, t2, ry, full,
    r_s, r_r, c_s, c_r, x_s, x_r, y_s, y_r, gy_s, gy_r, gx_s, gx_r, gc_s, gc_r,
):
    y, x, c, z = place()
    partner = device(y, x, 1 - c, z)
    x_dev = [device(y, (x + d) % NX, c, z) for d in range(NX)]
    y_dev = [device((y + d) % NY, x, c, z) for d in range(NY)]
    z_dev = [device(y, x, c, (z + NZ - d) % NZ) for d in range(NZ)]
    barrier = pltpu.get_barrier_semaphore()
    for dev in [partner] + x_dev[1:] + y_dev[1:] + z_dev[1:]:
        pl.semaphore_signal(barrier, inc=1, device_id=dev, device_id_type=MESH)

    expert_row = lax.broadcasted_iota(jnp.int32, (16, 256), 0)
    before = (
        lax.broadcasted_iota(jnp.int32, (256, 256), 0)
        < lax.broadcasted_iota(jnp.int32, (256, 256), 1)
    ).astype(F32).astype(BF)
    slot_row = lax.broadcasted_iota(jnp.int32, (CAPE, 256), 0).astype(F32)

    def one_row(table, e):
        return jnp.sum(jnp.where(expert_row == e, table, 0.0), 0, keepdims=True)

    def selector(hot, rank, e):
        return jnp.where(
            (slot_row == one_row(rank, e)) & (one_row(hot, e) > 0.5), 1.0, 0.0
        )

    def local(j):
        return 1 - c if j == 0 else c

    def home(k, carry):
        owner = (z + NZ - k) % NZ
        mine = att[:, pl.ds(pl.multiple_of(owner * 256, 256), 256)]
        stream = (res[k].astype(F32) + dot(mine, out_proj[...], TN)).astype(BF)
        wide = stream.astype(F32)
        inv = lax.rsqrt(jnp.mean(wide * wide, -1, keepdims=True) + norm_eps)
        normed = (wide * inv * gain[...]).astype(BF)
        gate = jax.nn.sigmoid(dot(router[...], normed, NT))
        listed = ids[k]
        hot = jnp.where(
            (listed[0:1] == expert_row) | (listed[1:2] == expert_row), 1.0, 0.0
        )
        rank = dot(hot.astype(BF), before)

        @pl.when(k == 0)
        def _():
            hot_own[...] = hot
            rank_own[...] = rank
            stream_own[...] = wide
            inv_own[...] = jnp.broadcast_to(inv, (256, 128))

        at = pl.ds(pl.multiple_of(k * CAPE, CAPE), CAPE)
        for j in range(2):
            e = 2 * z + local(j)
            picked = selector(hot, rank, e)
            picked_b = picked.astype(BF)
            rows[j, at, :] = dot(picked_b, normed).astype(BF)
            cots[j, at, :] = dot(picked_b, cot[k]).astype(BF)
            value = jnp.sum(picked * one_row(gate, e), 1, keepdims=True)
            gates[j, at, :] = jnp.broadcast_to(value, (CAPE, 128))
        return carry

    lax.fori_loop(0, NZ, home, 0)

    back = []
    for j in range(2):
        e = local(j)
        inp, outp = w_in[e], w_out[e]
        x_rows = rows[j]
        gate = gates[j][:, 0:1]
        cot_rows = cots[j].astype(F32)
        scaled = (gate * cot_rows).astype(BF)
        pre = dot(x_rows, inp)
        square = pre * pre
        t = jnp.tanh(root_two_pi * (pre + cubic_term * square * pre))
        hidden = (0.5 * pre * (1.0 + t)).astype(BF)
        slope = 0.5 * (1.0 + t) + 0.5 * pre * (1.0 - t * t) * root_two_pi * (
            1.0 + 3.0 * cubic_term * square
        )
        grad_pre = (dot(scaled, outp, NT) * slope).astype(BF)
        gb[j] = dot(hidden, scaled, TN).astype(BF)
        grad_in = dot(x_rows, grad_pre, TN).astype(BF)
        ga[j, 0:256, :] = grad_in[:, 0:256]
        ga[j, 256:512, :] = grad_in[:, 256:512]
        if j == 0:
            pl.semaphore_wait(barrier, 18)
            pair = [
                send(g.at[0], rc.at[i], c_s.at[i], c_r.at[i], partner)
                for i, g in enumerate((ga, gb))
            ]
        made = dot(hidden, outp)
        grad_rows = dot(grad_pre, inp, NT)
        grad_gate = jnp.sum(cot_rows * made, -1, keepdims=True)
        grad_logit = grad_gate * gate * (1.0 - gate)
        column = one_row(router[...].astype(F32), 2 * z + e)
        first = (gate * made).astype(BF)
        second = (grad_rows + grad_logit * column).astype(BF)
        for k in range(NZ):
            ret[j, k, :, 0:256] = first[k * CAPE : (k + 1) * CAPE]
            ret[j, k, :, 256:512] = second[k * CAPE : (k + 1) * CAPE]
        for k in (4, 3, 5, 2, 6, 1, 7):
            back.append(
                send(ret.at[j, k], rr.at[j, k], r_s.at[j, k], r_r.at[j, k], z_dev[k])
            )

    chains = range(2)
    sent = []
    over_x = [[], []]
    for i in chains:
        pair[i].wait_recv()
        own = ga if i == 0 else gb
        t1[i] = (own[1].astype(F32) + rc[i].astype(F32)).astype(BF)
        for d in (2, 1, 3):
            to = (x + d) % NX
            over_x[i].append(
                send(
                    t1.at[i, pl.ds(pl.multiple_of(to * 128, 128), 128)],
                    rx.at[i, d], x_s.at[i, d], x_r.at[i, d], x_dev[d],
                )
            )
    over_y = [[], []]
    for i in chains:
        total = t1[i, pl.ds(pl.multiple_of(x * 128, 128), 128), :].astype(F32)
        for copy in over_x[i]:
            copy.wait_recv()
        for d in range(1, NX):
            total += rx[i, d].astype(F32)
        t2[i] = total.astype(BF)
        for d in (4, 3, 5, 2, 6, 1, 7):
            to = (y + d) % NY
            over_y[i].append(
                send(
                    t2.at[i, pl.ds(pl.multiple_of(to * 16, 16), 16)],
                    ry.at[i, d], y_s.at[i, d], y_r.at[i, d], y_dev[d],
                )
            )
    def span(size):
        first = {16: x * 128 + y * 16, 128: x * 128, 512: 0}[size] + c * 512
        return pl.ds(pl.multiple_of(first, size), size)

    out_y = [[], []]
    for i in chains:
        total = t2[i, pl.ds(pl.multiple_of(y * 16, 16), 16), :].astype(F32)
        for copy in over_y[i]:
            copy.wait_recv()
        for d in range(1, NY):
            total += ry[i, d].astype(F32)
        full[i, span(16), :] = total.astype(BF)
        for d in (4, 3, 5, 2, 6, 1, 7):
            part = full.at[i, span(16)]
            out_y[i].append(send(part, part, gy_s.at[i, d], gy_r.at[i, d], y_dev[d]))
    out_x = [[], []]
    for i in chains:
        for copy in out_y[i]:
            copy.wait_recv()
        for d in (2, 1, 3):
            part = full.at[i, span(128)]
            out_x[i].append(send(part, part, gx_s.at[i, d], gx_r.at[i, d], x_dev[d]))

    for copy in back:
        copy.wait_recv()
    hot, rank = hot_own[...], rank_own[...]
    total = None
    for j in range(2):
        picks, parts = [], []
        for k in range(NZ):
            e = 2 * ((z + k) % NZ) + local(j)
            picks.append(selector(hot, rank, e).astype(BF))
            parts.append(ret[j, 0] if k == 0 else rr[j, k])
        part = dot(jnp.concatenate(picks, 0), jnp.concatenate(parts, 0), TN)
        total = part if total is None else total + part
    wide, inv = stream_own[...], inv_own[...][:, 0:1]
    layer_out[...] = (wide + total[:, 0:256]).astype(BF)
    gained = total[:, 256:512] * gain[...]
    mean = jnp.mean(wide * gained, -1, keepdims=True)
    grad_stream[...] = (
        cot[0].astype(F32) + inv * gained - wide * (inv * inv * inv) * mean
    ).astype(BF)

    out_c = []
    for i in chains:
        for copy in out_x[i]:
            copy.wait_recv()
        part = full.at[i, span(512)]
        out_c.append(send(part, part, gc_s.at[i], gc_r.at[i], partner))
    for copy in out_c:
        copy.wait_recv()
    grads[...] = full[...]
    for copy in pair + back + out_c:
        copy.wait_send()
    for group in (over_x, over_y, out_y, out_x):
        for i in chains:
            for copy in group[i]:
                copy.wait_send()


VM = pl.BlockSpec(memory_space=pltpu.VMEM)
SM = pl.BlockSpec(memory_space=pltpu.SMEM)
DMA = pltpu.SemaphoreType.DMA


def exchange(idx, wtab, kv, q, res, cot, ids):
    return pl.pallas_call(
        exchange_kernel,
        name="exchange",
        out_shape=(
            jax.ShapeDtypeStruct((256, 2048), BF),
            jax.ShapeDtypeStruct((8, 256, 256), BF),
            jax.ShapeDtypeStruct((8, 256, 256), BF),
            jax.ShapeDtypeStruct((8, 8, 256), jnp.int32),
        ),
        in_specs=[SM] + [VM] * 6,
        out_specs=(VM,) * 4,
        scratch_shapes=[pltpu.VMEM((16, 64, 128), BF)] * 7
        + [
            pltpu.VMEM((8, 256, 256), BF),
            pltpu.VMEM((8, 256, 256), BF),
            pltpu.VMEM((8, 8, 256), jnp.int32),
            pltpu.VMEM((8, 8, 128), jnp.int32),
            pltpu.SMEM((8, 8, 128), jnp.int32),
            pltpu.VMEM((8, 8, 2, 64, 128), BF),
            pltpu.VMEM((128, 64, 128), BF),
            pltpu.VMEM((8, 4, 32, 512), BF),
            DMA((2, 8)), DMA((2, 8)), DMA((3, 8)), DMA((3, 8)),
            DMA((8,)), DMA((8,)), DMA((8, 8)), DMA((8, 8)),
            DMA((4, 8)), DMA((4, 8)), DMA((2,)),
        ],
        compiler_params=pltpu.CompilerParams(
            collective_id=0, has_side_effects=True, vmem_limit_bytes=40 << 20
        ),
    )(idx, wtab, kv, q, res, cot, ids)


def experts(*args):
    return pl.pallas_call(
        expert_kernel,
        name="experts",
        out_shape=(
            jax.ShapeDtypeStruct((2, 1024, 256), BF),
            jax.ShapeDtypeStruct((256, 256), BF),
            jax.ShapeDtypeStruct((256, 256), BF),
        ),
        in_specs=[VM] * 9,
        out_specs=(VM,) * 3,
        scratch_shapes=[
            pltpu.VMEM((2, 512, 256), BF),
            pltpu.VMEM((2, 512, 256), BF),
            pltpu.VMEM((2, 512, 128), F32),
            pltpu.VMEM((2, 512, 256), BF),
            pltpu.VMEM((2, 512, 256), BF),
            pltpu.VMEM((2, 8, CAPE, 512), BF),
            pltpu.VMEM((2, 8, CAPE, 512), BF),
            pltpu.VMEM((16, 256), F32),
            pltpu.VMEM((16, 256), F32),
            pltpu.VMEM((256, 256), F32),
            pltpu.VMEM((256, 128), F32),
            pltpu.VMEM((2, 512, 256), BF),
            pltpu.VMEM((2, 512, 256), BF),
            pltpu.VMEM((2, 4, 128, 256), BF),
            pltpu.VMEM((2, 128, 256), BF),
            pltpu.VMEM((2, 8, 16, 256), BF),
            pltpu.VMEM((2, 1024, 256), BF),
            DMA((2, 8)), DMA((2, 8)), DMA((2,)), DMA((2,)),
            DMA((2, 4)), DMA((2, 4)), DMA((2, 8)), DMA((2, 8)),
            DMA((2, 8)), DMA((2, 8)), DMA((2, 4)), DMA((2, 4)),
            DMA((2,)), DMA((2,)),
        ],
        compiler_params=pltpu.CompilerParams(
            collective_id=1, has_side_effects=True, vmem_limit_bytes=44 << 20
        ),
    )(*args)


def tables(block_list):
    y, x, c, _ = place()
    asked = block_list.reshape(-1)
    owner, inner = asked // 16, asked % 16
    entry = jnp.arange(64, dtype=jnp.int32)
    earlier = (owner[:, None] == owner[None, :]) & (entry[None, :] < entry[:, None])
    rank = jnp.sum(earlier.astype(jnp.int32), 1)
    owner_y, line = owner // (NX * NC), owner % (NX * NC)
    rows = jnp.arange(8, dtype=jnp.int32)[:, None, None]
    lanes = jnp.arange(128, dtype=jnp.int32)[None, :, None]
    hit = (owner_y[None, None, :] == rows) & ((line * 2 + rank)[None, None, :] == lanes)
    wanted = jnp.sum(jnp.where(hit, inner[None, None, :], 0), -1)
    supplier = (x - line // NC) % NX * NC + (c - line % NC) % NC
    index = (supplier * 8 + (owner_y - y) % NY) * 2 + rank
    return index, wanted


def shards(
    query_cols, key_cols, value_cols, block_list, residual, out_proj, norm_gain,
    router_weight, expert_ids, expert_in, expert_out, cotangent,
):
    index, wanted = tables(block_list)
    pairs = jnp.concatenate([key_cols, value_cols], 0).reshape(64, 16, 128)
    ids = jnp.pad(expert_ids.T, ((0, 6), (0, 0)))
    att, res, cot, listed = exchange(
        index, wanted, jnp.transpose(pairs, (1, 0, 2)), query_cols, residual, cotangent, ids
    )
    grads, layer_out, grad_stream = experts(
        att, res, cot, listed, out_proj, norm_gain.reshape(1, 256), router_weight.T,
        expert_in, expert_out,
    )
    wide = grads.astype(F32)
    grad_in = jnp.transpose(wide[0].reshape(2, 2, 256, 256), (0, 2, 1, 3)).reshape(2, 256, 512)
    return layer_out, grad_stream, grad_in, wide[1].reshape(2, 512, 256)


def solution(mesh):
    assert (mesh.shape["seq"], mesh.shape["expert"]) == (NY * NX * NC, NZ)
    return jax.shard_map(
        shards,
        mesh=mesh,
        in_specs=(
            P("expert", "seq"),
            P("expert", "seq"),
            P("expert", "seq"),
            P("seq", None),
            P(("seq", "expert"), None),
            P(),
            P(),
            P(),
            P(("seq", "expert"), None),
            P("expert", None, None),
            P("expert", None, None),
            P(("seq", "expert"), None),
        ),
        out_specs=(
            P(("seq", "expert"), None),
            P(("seq", "expert"), None),
            P("expert", None, None),
            P("expert", None, None),
        ),
        check_vma=False,
    )
```

```python
import math

import jax
import jax.numpy as jnp
from jax import lax
from jax.experimental import pallas as pl
from jax.experimental.pallas import tpu as pltpu
from jax.sharding import PartitionSpec as P

MESH = pl.DeviceIdType.MESH
BF = jnp.bfloat16
F32 = jnp.float32
HD = 32
NY, NX, NC, NZ = 8, 4, 2, 8
CAPE = 64

norm_eps = 1e-05
root_two_pi = 0.7978845608028654
cubic_term = 0.044715

TN = (((0,), (0,)), ((), ()))
NT = (((1,), (1,)), ((), ()))


def dot(a, b, dims=(((1,), (0,)), ((), ()))):
    return lax.dot_general(a, b, dims, preferred_element_type=F32)


def place():
    seq, z = lax.axis_index("seq"), lax.axis_index("expert")
    y = seq // (NX * NC)
    x = (seq // NC) % NX
    c = seq % NC
    return y, x, c, z


def device(y, x, c, z):
    return ((y * NX + x) * NC + c, z)


def send(src, dst, ssem, rsem, dev):
    copy = pltpu.make_async_remote_copy(
        src_ref=src, dst_ref=dst, send_sem=ssem, recv_sem=rsem, device_id=dev, device_id_type=MESH
    )
    copy.start()
    return copy


class Ring:
    def __init__(self, slots, ssem, rsem, up, down, far_up):
        self.slots, self.ssem, self.rsem = slots, ssem, rsem
        self.up, self.down, self.far_up = up, down, far_up
        self.copies = {}

    def go(self, frm, to, dev):
        self.copies[to] = send(self.slots(frm), self.slots(to), self.ssem(to), self.rsem(to), dev)

    def begin(self):
        self.go(0, 1, self.up)
        self.go(0, 7, self.down)

    def arrive(self, k):
        self.copies[k].wait_recv()
        if k < 3 or (k == 3 and self.far_up):
            self.go(k, k + 1, self.up)
        if k > 5 or (k == 5 and not self.far_up):
            self.go(k, k - 1, self.down)


def drain(ref, sem):
    pltpu.make_async_copy(ref, ref, sem).wait()


def layer_kernel(
    idx, wtab, ids, gain, router, k_hbm, v_hbm, q_hbm, res_hbm, cot_hbm, op_hbm, wi_hbm, wo_hbm,
    grads, layer_out, grad_stream,
    yb0, yb1, yb2, yb3, yb4, yb5, yb6, yb7,
    zr, zc, zi, wr, wsm, sb, rv, at, q, op, opp, w_in, w_out,
    before, sel, pk, rows, cots, gates, ga, gb, ret, rr, stream_own, inv_own,
    rc, t1, rx, t2, ry, full,
    cols, kv_l, m_l, y_s, y_r, z_s, z_r, w_s, w_r, x_s, x_r, a_s, a_r,
    r_s, r_r, c_s, c_r, gx_s, gx_r, gy_s, gy_r, hy_s, hy_r, hx_s, hx_r, hc_s, hc_r,
):
    y, x, c, z = place()
    row = [(dx, dc) for dx in range(NX) for dc in range(NC)]
    peers = [device(y, (x + dx) % NX, (c + dc) % NC, z) for dx, dc in row]
    partner = peers[1]
    x_dev = [device(y, (x + d) % NX, c, z) for d in range(NX)]
    y_dev = [device((y + d) % NY, x, c, z) for d in range(NY)]
    z_dev = [device(y, x, c, (z + NZ - d) % NZ) for d in range(NZ)]
    up_y, down_y = y_dev[1], y_dev[7]
    up_z, down_z = z_dev[7], z_dev[1]

    barrier = pltpu.get_barrier_semaphore()
    for dev in z_dev[1:] + y_dev[1:] + peers[1:]:
        pl.semaphore_signal(barrier, inc=1, device_id=dev, device_id_type=MESH)

    def fetch(src, dst, sem):
        copy = pltpu.make_async_copy(src, dst, sem)
        copy.start()
        return copy

    fetched = [fetch(k_hbm, cols.at[0], kv_l.at[0]), fetch(v_hbm, cols.at[1], kv_l.at[1])]
    got_res = fetch(res_hbm, zr.at[0], m_l.at[0])
    got_cot = fetch(cot_hbm, zc.at[0], m_l.at[1])
    later = [
        fetch(a, v, m_l.at[2 + i])
        for i, (a, v) in enumerate(((q_hbm, q), (op_hbm, op), (wi_hbm, w_in), (wo_hbm, w_out)))
    ]
    own_table = fetch(wtab, wsm.at[0], m_l.at[6])
    before[...] = jnp.where(
        lax.broadcasted_iota(jnp.int32, (256, 256), 0)
        < lax.broadcasted_iota(jnp.int32, (256, 256), 1),
        1.0,
        0.0,
    ).astype(BF)
    for i in range(2):
        fetched[i].wait()
        for n in range(16):
            yb0[n, i * HD : (i + 1) * HD, :] = cols[i, :, n * 128 : (n + 1) * 128]
    got_res.wait()
    got_cot.wait()
    pl.semaphore_wait(barrier, 21)

    ybs = [yb0, yb1, yb2, yb3, yb4, yb5, yb6, yb7]
    for r in range(1, 8):
        send(wtab, wr.at[r], w_s.at[0], w_r.at[0], peers[r])

    def y_ring(ch):
        return Ring(
            lambda k: ybs[k].at[pl.ds(ch * 4, 4)],
            lambda k: y_s.at[0],
            lambda k: y_r.at[ch, k - 1],
            up_y, down_y, ch < 2,
        )

    def z_ring(i, slots, far_up):
        return Ring(
            slots, lambda k: z_s.at[i // 2], lambda k: z_r.at[i, k - 1], up_z, down_z, far_up
        )

    def half(buf, h):
        return lambda k: buf.at[k, pl.ds(h * 128, 128)]

    ys = [y_ring(ch) for ch in range(4)]
    zs = [
        z_ring(0, half(zr, 0), True),
        z_ring(1, half(zr, 1), False),
        z_ring(2, half(zc, 0), True),
        z_ring(3, half(zc, 1), False),
    ]
    zids = z_ring(4, lambda k: ids if k == 0 else zi.at[k], True)
    zids.begin()
    for ch in range(4):
        ys[ch].begin()
        zs[ch].begin()

    drain(wr.at[pl.ds(1, 7)], w_r.at[0])
    rest = fetch(wr.at[pl.ds(1, 7)], wsm.at[pl.ds(1, 7)], m_l.at[7])
    own_table.wait()
    rest.wait()

    line = x * NC + c

    def pick(rel):
        source = ybs[(8 - rel) % 8]
        owner_row = (y + rel) % NY
        for r in (4, 5, 2, 3, 6, 7, 1, 0):
            dx, dc = row[r]
            asked = ((NX - dx) % NX) * NC + dc
            for s in range(2):
                block = wsm[asked, owner_row, line * 2 + s]
                if r == 0:
                    rv[rel * 2 + s] = source[block]
                else:
                    sb[rel, r - 1, s] = source[block]
            if r:
                send(
                    sb.at[rel, r - 1],
                    rv.at[pl.ds((r * 8 + rel) * 2, 2)],
                    x_s.at[0],
                    x_r.at[0],
                    peers[r],
                )

    expert_row = lax.broadcasted_iota(jnp.int32, (16, 256), 0)
    slot_row = lax.broadcasted_iota(jnp.int32, (CAPE, 256), 0).astype(F32)

    def one_row(table, e):
        return jnp.sum(jnp.where(expert_row == e, table, 0.0), 0, keepdims=True)

    def local(j):
        return 1 - c if j == 0 else c

    def prepare(k):
        listed = ids[...] if k == 0 else zi[k]
        hot = jnp.where(
            (listed[0:1] == expert_row) | (listed[1:2] == expert_row), 1.0, 0.0
        )
        rank = dot(hot.astype(BF), before[...])
        place_of = jnp.where(hot > 0.5, rank, -1.0)

        def selector(e):
            return jnp.where(slot_row == one_row(place_of, e), 1.0, 0.0).astype(BF)

        for j in range(2):
            picked = selector(2 * z + local(j))
            sel[j, k] = picked
            cots[j, k * CAPE : (k + 1) * CAPE, :] = dot(picked, zc[k]).astype(BF)
        if k == 0:
            for j in range(2):
                for d in range(NZ):
                    pk[j, d * CAPE : (d + 1) * CAPE, :] = selector(
                        2 * ((z + d) % NZ) + local(j)
                    )

    pick(0)
    for copy in later:
        copy.wait()
    for k in range(NZ):
        head = (z + NZ - k) % NZ
        opp[k * HD : (k + 1) * HD, :] = op[pl.ds(pl.multiple_of(head * HD, HD), HD), :]
    prepare(0)
    for k in (1, 2, 3):
        for ch in range(4):
            for slot in (k, 8 - k):
                ys[ch].arrive(slot)
                zs[ch].arrive(slot)
        for slot in (k, 8 - k):
            zids.arrive(slot)
            pick((8 - slot) % 8)
        for slot in (k, 8 - k):
            prepare(slot)
    for ring in ys:
        ring.arrive(4)
    pick(4)
    for ring in zs + [zids]:
        ring.arrive(4)
    prepare(4)
    drain(rv.at[pl.ds(16, 112)], x_r.at[0])

    rings = []

    def attend(ch):
        def block(i, carry):
            b = ch * 4 + i
            pairs = [rv[idx[b * 4 + j]] for j in range(4)]
            keys = jnp.concatenate([p[:HD] for p in pairs], 1)
            values = jnp.concatenate([p[HD:] for p in pairs], 1)
            queries = q[:, pl.ds(pl.multiple_of(b * 128, 128), 128)]
            scores = dot(keys, queries, TN) * (1.0 / math.sqrt(HD))
            weights = jnp.exp(scores - jnp.max(scores, 0, keepdims=True))
            total = jnp.sum(weights, 0, keepdims=True)
            out = dot(values, weights.astype(BF)) / total
            at[0, ch, :, pl.ds(pl.multiple_of(i * 128, 128), 128)] = out.astype(BF)
            return carry

        lax.fori_loop(0, 4, block, 0, unroll=True)
        ring = Ring(
            lambda k: at.at[k, ch],
            lambda k: a_s.at[0],
            lambda k: a_r.at[ch, k - 1],
            up_z, down_z, ch < 2,
        )
        ring.begin()
        rings.append(ring)

    def arrive(k, ch):
        rings[ch].arrive(k)
        if k < 4:
            rings[ch].arrive(8 - k)

    def home(ch):
        mixed = at[:, ch].reshape(256, 512)
        projected = dot(mixed, opp[...], TN)
        for i in range(2):
            k = (z + NZ - (2 * ch + i)) % NZ
            stream = (zr[k].astype(F32) + projected[i * 256 : (i + 1) * 256]).astype(BF)
            wide = stream.astype(F32)
            inv = lax.rsqrt(jnp.mean(wide * wide, -1, keepdims=True) + norm_eps)
            normed = (wide * inv * gain[...]).astype(BF)
            gate = jax.nn.sigmoid(dot(router[...], normed, NT))

            @pl.when(k == 0)
            def _():
                stream_own[...] = wide
                inv_own[...] = jnp.broadcast_to(inv, (256, 128))

            at_rows = pl.ds(pl.multiple_of(k * CAPE, CAPE), CAPE)
            for j in range(2):
                picked = sel[j, k]
                rows[j, at_rows, :] = dot(picked, normed).astype(BF)
                value = jnp.sum(
                    picked.astype(F32) * one_row(gate, 2 * z + local(j)), 1, keepdims=True
                )
                gates[j, at_rows, :] = jnp.broadcast_to(value, (CAPE, 128))

    attend(0)
    attend(1)
    attend(2)
    arrive(1, 0)
    attend(3)
    for k, ch in (
        (1, 1), (2, 0), (1, 2), (2, 1), (1, 3), (3, 0), (2, 2), (3, 1), (2, 3), (4, 0), (3, 2),
    ):
        arrive(k, ch)
    home(0)
    arrive(4, 1)
    arrive(3, 3)
    home(1)
    arrive(4, 2)
    home(2)
    arrive(4, 3)
    home(3)

    chains = range(2)

    def cross_x(i):
        pair[i].wait_recv()
        own = ga if i == 0 else gb
        t1[i] = (own[1].astype(F32) + rc[i].astype(F32)).astype(BF)
        for d in (2, 1, 3):
            to = (x + d) % NX
            send(
                t1.at[i, pl.ds(pl.multiple_of(to * 128, 128), 128)],
                rx.at[i, d], gx_s.at[i], gx_r.at[i], x_dev[d],
            )

    for j in range(2):
        e = local(j)
        inp, outp = w_in[e], w_out[e]
        x_rows = rows[j]
        gate = gates[j][:, 0:1]
        cot_rows = cots[j].astype(F32)
        scaled = (gate * cot_rows).astype(BF)
        pre = dot(x_rows, inp)
        grad_hidden = dot(scaled, outp, NT)
        square = pre * pre
        half_up = 0.5 + 0.5 * jnp.tanh(pre * (root_two_pi + root_two_pi * cubic_term * square))
        hidden = (pre * half_up).astype(BF)
        slope = half_up * (
            1.0
            + (1.0 - half_up) * pre * (2.0 * root_two_pi + 6.0 * root_two_pi * cubic_term * square)
        )
        grad_pre = (grad_hidden * slope).astype(BF)

        def weights_part():
            gb[j] = dot(hidden, scaled, TN).astype(BF)
            grad_in = dot(x_rows, grad_pre, TN).astype(BF)
            ga[j, 0:256, :] = grad_in[:, 0:256]
            ga[j, 256:512, :] = grad_in[:, 256:512]

        def rows_part():
            made = dot(hidden, outp)
            grad_rows = dot(grad_pre, inp, NT)
            grad_gate = jnp.sum(cot_rows * made, -1, keepdims=True)
            grad_logit = grad_gate * gate * (1.0 - gate)
            column = one_row(router[...].astype(F32), 2 * z + e)
            first = (gate * made).astype(BF)
            second = (grad_rows + grad_logit * column).astype(BF)
            for k in (4, 3, 5, 2, 6, 1, 7, 0):
                target = ret if k else rr
                target[j, k, :, 0:256] = first[k * CAPE : (k + 1) * CAPE]
                target[j, k, :, 256:512] = second[k * CAPE : (k + 1) * CAPE]
                if k:
                    send(ret.at[j, k], rr.at[j, k], r_s.at[j], r_r.at[j], z_dev[k])

        if j == 0:
            rows_part()
            weights_part()
            pair = [
                send(g.at[0], rc.at[i], c_s.at[i], c_r.at[i], partner)
                for i, g in enumerate((ga, gb))
            ]
        else:
            weights_part()
            for i in chains:
                cross_x(i)
            rows_part()

    for i in chains:
        total = t1[i, pl.ds(pl.multiple_of(x * 128, 128), 128), :].astype(F32)
        drain(rx.at[i, pl.ds(1, 3)], gx_r.at[i])
        for d in range(1, NX):
            total += rx[i, d].astype(F32)
        t2[i] = total.astype(BF)
        for d in (4, 3, 5, 2, 6, 1, 7):
            to = (y + d) % NY
            send(
                t2.at[i, pl.ds(pl.multiple_of(to * 16, 16), 16)],
                ry.at[i, d], gy_s.at[i], gy_r.at[i], y_dev[d],
            )

    def span(size):
        first = {16: x * 128 + y * 16, 128: x * 128, 512: 0}[size] + c * 512
        return pl.ds(pl.multiple_of(first, size), size)

    for i in chains:
        total = t2[i, pl.ds(pl.multiple_of(y * 16, 16), 16), :].astype(F32)
        drain(ry.at[i, pl.ds(1, 7)], gy_r.at[i])
        for d in range(1, NY):
            total += ry[i, d].astype(F32)
        full[i, span(16), :] = total.astype(BF)
        for d in (4, 3, 5, 2, 6, 1, 7):
            part = full.at[i, span(16)]
            send(part, part, hy_s.at[i], hy_r.at[i], y_dev[d])
    for i in chains:
        drain(ry.at[i, pl.ds(1, 7)], hy_r.at[i])
        for d in (2, 1, 3):
            part = full.at[i, span(128)]
            send(part, part, hx_s.at[i], hx_r.at[i], x_dev[d])

    def gathered(j):
        return dot(pk[j], rr[j].reshape(512, 512), TN)

    drain(rr.at[0, pl.ds(1, 7)], r_r.at[0])
    total = gathered(0)
    out_c = []
    for i in chains:
        drain(rx.at[i, pl.ds(1, 3)], hx_r.at[i])
        part = full.at[i, span(512)]
        out_c.append(send(part, part, hc_s.at[i], hc_r.at[i], partner))
    for copy in out_c:
        copy.wait_recv()
    kept = fetch(full, grads, m_l.at[8])

    drain(rr.at[1, pl.ds(1, 7)], r_r.at[1])
    total += gathered(1)
    wide, inv = stream_own[...], inv_own[...][:, 0:1]
    layer_out[...] = (wide + total[:, 0:256]).astype(BF)
    gained = total[:, 256:512] * gain[...]
    mean = jnp.mean(wide * gained, -1, keepdims=True)
    grad_stream[...] = (
        zc[0].astype(F32) + inv * gained - wide * (inv * inv * inv) * mean
    ).astype(BF)

    kept.wait()
    drain(wr.at[pl.ds(1, 7)], w_s.at[0])
    drain(rv.at[pl.ds(16, 112)], y_s.at[0])
    drain(zr.at[pl.ds(1, 7)], z_s.at[0])
    drain(zc.at[pl.ds(1, 7)], z_s.at[1])
    drain(zi.at[pl.ds(1, 7)], z_s.at[2])
    drain(sb, x_s.at[0])
    drain(at.at[pl.ds(1, 7)], a_s.at[0])
    for copy in pair + out_c:
        copy.wait_send()
    for i in chains:
        drain(ret.at[i, pl.ds(1, 7)], r_s.at[i])
        drain(rx.at[i, pl.ds(1, 3)], gx_s.at[i])
        drain(ry.at[i, pl.ds(1, 7)], gy_s.at[i])
        drain(ry.at[i, pl.ds(1, 7)], hy_s.at[i])
        drain(rx.at[i, pl.ds(1, 3)], hx_s.at[i])


VM = pl.BlockSpec(memory_space=pltpu.VMEM)
SM = pl.BlockSpec(memory_space=pltpu.SMEM)
HB = pl.BlockSpec(memory_space=pltpu.HBM)
DMA = pltpu.SemaphoreType.DMA


def layer(*args):
    def vm(*shape, dtype=BF):
        return pltpu.VMEM(shape, dtype)

    return pl.pallas_call(
        layer_kernel,
        name="layer",
        out_shape=(
            jax.ShapeDtypeStruct((2, 1024, 256), BF),
            jax.ShapeDtypeStruct((256, 256), BF),
            jax.ShapeDtypeStruct((256, 256), BF),
        ),
        in_specs=[SM] + [VM] * 4 + [HB] * 8,
        out_specs=(HB, VM, VM),
        scratch_shapes=[vm(16, 64, 128)] * 8
        + [
            vm(8, 256, 256), vm(8, 256, 256), vm(8, 2, 256, dtype=jnp.int32),
            vm(8, 8, 128, dtype=jnp.int32), pltpu.SMEM((8, 8, 128), jnp.int32),
            vm(8, 7, 2, 64, 128), vm(128, 64, 128), vm(8, 4, 32, 512),
            vm(32, 2048), vm(256, 256), vm(256, 256), vm(2, 256, 512), vm(2, 512, 256),
            vm(256, 256), vm(2, 8, CAPE, 256), vm(2, 512, 256),
            vm(2, 512, 256), vm(2, 512, 256), vm(2, 512, 128, dtype=F32),
            vm(2, 512, 256), vm(2, 512, 256), vm(2, 8, CAPE, 512), vm(2, 8, CAPE, 512),
            vm(256, 256, dtype=F32), vm(256, 128, dtype=F32),
            vm(2, 512, 256), vm(2, 512, 256), vm(2, 4, 128, 256),
            vm(2, 128, 256), vm(2, 8, 16, 256), vm(2, 1024, 256),
            vm(2, 32, 2048), DMA((2,)), DMA((9,)), DMA((1,)), DMA((4, 7)), DMA((3,)), DMA((5, 7)),
            DMA((1,)), DMA((1,)), DMA((1,)), DMA((1,)), DMA((1,)), DMA((4, 7)),
        ]
        + [DMA((2,))] * 14,
        compiler_params=pltpu.CompilerParams(
            collective_id=0, has_side_effects=True, vmem_limit_bytes=66_000_000
        ),
    )(*args)


def widen_kernel(
    grads, layer_in, grad_in, ga, gb, layer_out, grad_out, held, wide_a, wide_b, rows, i_s, o_s
):
    loads = [
        pltpu.make_async_copy(
            grads.at[i, pl.ds(e * 512, 512)], held.at[i, e], i_s.at[2 * i + e]
        )
        for i in range(2)
        for e in range(2)
    ]
    loads += [
        pltpu.make_async_copy(layer_in, rows.at[0], i_s.at[4]),
        pltpu.make_async_copy(grad_in, rows.at[1], i_s.at[5]),
    ]
    for load in loads:
        load.start()
    stores = []
    for n, load in enumerate(loads):
        load.wait()
        i, e = n // 2, n % 2
        if i == 0:
            wide_a[e, :, 0:256] = held[0, e, 0:256].astype(F32)
            wide_a[e, :, 256:512] = held[0, e, 256:512].astype(F32)
            pair = (wide_a.at[e], ga.at[e])
        elif i == 1:
            wide_b[e] = held[1, e].astype(F32)
            pair = (wide_b.at[e], gb.at[e])
        else:
            pair = (rows.at[e], (layer_out, grad_out)[e])
        store = pltpu.make_async_copy(pair[0], pair[1], o_s.at[n])
        store.start()
        stores.append(store)
    for store in stores:
        store.wait()


def widen(*args):
    return pl.pallas_call(
        widen_kernel,
        name="widen",
        out_shape=(
            jax.ShapeDtypeStruct((2, 256, 512), F32),
            jax.ShapeDtypeStruct((2, 512, 256), F32),
            jax.ShapeDtypeStruct((256, 256), BF),
            jax.ShapeDtypeStruct((256, 256), BF),
        ),
        in_specs=[HB] * 3,
        out_specs=(HB,) * 4,
        scratch_shapes=[
            pltpu.VMEM((2, 2, 512, 256), BF),
            pltpu.VMEM((2, 256, 512), F32),
            pltpu.VMEM((2, 512, 256), F32),
            pltpu.VMEM((2, 256, 256), BF),
            DMA((6,)),
            DMA((6,)),
        ],
        compiler_params=pltpu.CompilerParams(vmem_limit_bytes=66_000_000),
    )(*args)


def tables(block_list):
    y, x, c, _ = place()
    asked = block_list.reshape(-1)
    owner, inner = asked // 16, asked % 16
    entry = jnp.arange(64, dtype=jnp.int32)
    earlier = (owner[:, None] == owner[None, :]) & (entry[None, :] < entry[:, None])
    rank = jnp.sum(earlier.astype(jnp.int32), 1)
    owner_y, line = owner // (NX * NC), owner % (NX * NC)
    rows = jnp.arange(8, dtype=jnp.int32)[:, None, None]
    lanes = jnp.arange(128, dtype=jnp.int32)[None, :, None]
    hit = (owner_y[None, None, :] == rows) & ((line * 2 + rank)[None, None, :] == lanes)
    wanted = jnp.sum(jnp.where(hit, inner[None, None, :], 0), -1)
    supplier = (x - line // NC) % NX * NC + (c - line % NC) % NC
    index = (supplier * 8 + (owner_y - y) % NY) * 2 + rank
    return index, wanted


def shards(
    query_cols, key_cols, value_cols, block_list, residual, out_proj, norm_gain,
    router_weight, expert_ids, expert_in, expert_out, cotangent,
):
    index, wanted = tables(block_list)
    grads, layer_out, grad_stream = layer(
        index, wanted, expert_ids.T, norm_gain.reshape(1, 256), router_weight.T,
        key_cols, value_cols, query_cols, residual, cotangent, out_proj, expert_in, expert_out,
    )
    grad_in, grad_out, layer_out, grad_stream = widen(grads, layer_out, grad_stream)
    return layer_out, grad_stream, grad_in, grad_out


def solution(mesh):
    assert (mesh.shape["seq"], mesh.shape["expert"]) == (NY * NX * NC, NZ)
    return jax.shard_map(
        shards,
        mesh=mesh,
        in_specs=(
            P("expert", "seq"),
            P("expert", "seq"),
            P("expert", "seq"),
            P("seq", None),
            P(("seq", "expert"), None),
            P(),
            P(),
            P(),
            P(("seq", "expert"), None),
            P("expert", None, None),
            P("expert", None, None),
            P(("seq", "expert"), None),
        ),
        out_specs=(
            P(("seq", "expert"), None),
            P(("seq", "expert"), None),
            P("expert", None, None),
            P("expert", None, None),
        ),
        check_vma=False,
    )
```

```python
import math

import jax
import jax.numpy as jnp
from jax import lax
from jax.experimental import pallas as pl
from jax.experimental.pallas import tpu as pltpu
from jax.sharding import PartitionSpec as P

MESH = pl.DeviceIdType.MESH
BF = jnp.bfloat16
F32 = jnp.float32
HD = 32
NY, NX, NC, NZ = 8, 4, 2, 8
CAPE = 64

norm_eps = 1e-05
root_two_pi = 0.7978845608028654
cubic_term = 0.044715

TN = (((0,), (0,)), ((), ()))
NT = (((1,), (1,)), ((), ()))


def dot(a, b, dims=(((1,), (0,)), ((), ()))):
    return lax.dot_general(a, b, dims, preferred_element_type=F32)


def place():
    seq, z = lax.axis_index("seq"), lax.axis_index("expert")
    y = seq // (NX * NC)
    x = (seq // NC) % NX
    c = seq % NC
    return y, x, c, z


def device(y, x, c, z):
    return ((y * NX + x) * NC + c, z)


def send(src, dst, ssem, rsem, dev):
    copy = pltpu.make_async_remote_copy(
        src_ref=src, dst_ref=dst, send_sem=ssem, recv_sem=rsem, device_id=dev, device_id_type=MESH
    )
    copy.start()
    return copy


class Ring:
    def __init__(self, slots, ssem, rsem, up, down, far_up):
        self.slots, self.ssem, self.rsem = slots, ssem, rsem
        self.up, self.down, self.far_up = up, down, far_up
        self.copies = {}

    def go(self, frm, to, dev):
        self.copies[to] = send(self.slots(frm), self.slots(to), self.ssem(to), self.rsem(to), dev)

    def begin(self):
        self.go(0, 1, self.up)
        self.go(0, 7, self.down)

    def arrive(self, k):
        self.copies[k].wait_recv()
        if k < 3 or (k == 3 and self.far_up):
            self.go(k, k + 1, self.up)
        if k > 5 or (k == 5 and not self.far_up):
            self.go(k, k - 1, self.down)


def drain(ref, sem):
    pltpu.make_async_copy(ref, ref, sem).wait()


def layer_kernel(
    idx, wtab, ids, gain, router, k_hbm, v_hbm, q_hbm, res_hbm, cot_hbm, op_hbm, wi_hbm, wo_hbm,
    grads, layer_out, grad_stream,
    yb0, yb1, yb2, yb3, yb4, yb5, yb6, yb7,
    zr, zc, zi, wr, wsm, sb, rv, at, q, op, opp, w_in, w_out,
    before, sel, pk, rows, cots, ga, gb, ret, rr,
    rc, t1, rx, t2, ry, full,
    cols, kv_l, m_l, y_s, y_r, z_s, z_r, w_s, w_r, x_s, x_r, a_s, a_r,
    r_s, r_r, c_s, c_r, gx_s, gx_r, gy_s, gy_r, hy_s, hy_r, hx_s, hx_r, hc_s, hc_r,
):
    y, x, c, z = place()
    row = [(dx, dc) for dx in range(NX) for dc in range(NC)]
    peers = [device(y, (x + dx) % NX, (c + dc) % NC, z) for dx, dc in row]
    partner = peers[1]
    x_dev = [device(y, (x + d) % NX, c, z) for d in range(NX)]
    y_dev = [device((y + d) % NY, x, c, z) for d in range(NY)]
    z_dev = [device(y, x, c, (z + NZ - d) % NZ) for d in range(NZ)]
    up_y, down_y = y_dev[1], y_dev[7]
    up_z, down_z = z_dev[7], z_dev[1]

    barrier = pltpu.get_barrier_semaphore()
    for dev in z_dev[1:] + y_dev[1:] + peers[1:]:
        pl.semaphore_signal(barrier, inc=1, device_id=dev, device_id_type=MESH)

    def fetch(src, dst, sem):
        copy = pltpu.make_async_copy(src, dst, sem)
        copy.start()
        return copy

    fetched = [fetch(k_hbm, cols.at[0], kv_l.at[0]), fetch(v_hbm, cols.at[1], kv_l.at[1])]
    got_res = fetch(res_hbm, zr.at[0], m_l.at[0])
    got_cot = fetch(cot_hbm, zc.at[0], m_l.at[1])
    later = [
        fetch(a, v, m_l.at[2 + i])
        for i, (a, v) in enumerate(((q_hbm, q), (op_hbm, op), (wi_hbm, w_in), (wo_hbm, w_out)))
    ]
    own_table = fetch(wtab, wsm.at[0], m_l.at[6])
    before[...] = jnp.where(
        lax.broadcasted_iota(jnp.int32, (256, 256), 0)
        < lax.broadcasted_iota(jnp.int32, (256, 256), 1),
        1.0,
        0.0,
    ).astype(BF)
    for i in range(2):
        fetched[i].wait()
        for n in range(16):
            yb0[n, i * HD : (i + 1) * HD, :] = cols[i, :, n * 128 : (n + 1) * 128]
    got_res.wait()
    got_cot.wait()
    pl.semaphore_wait(barrier, 21)

    ybs = [yb0, yb1, yb2, yb3, yb4, yb5, yb6, yb7]
    for r in range(1, 8):
        send(wtab, wr.at[r], w_s.at[0], w_r.at[0], peers[r])

    def y_ring(ch):
        return Ring(
            lambda k: ybs[k].at[pl.ds(ch * 4, 4)],
            lambda k: y_s.at[0],
            lambda k: y_r.at[ch, k - 1],
            up_y, down_y, ch < 2,
        )

    def z_ring(i, slots, far_up):
        return Ring(
            slots, lambda k: z_s.at[i // 2], lambda k: z_r.at[i, k - 1], up_z, down_z, far_up
        )

    def half(buf, h):
        return lambda k: buf.at[k, pl.ds(h * 128, 128)]

    ys = [y_ring(ch) for ch in range(4)]
    zs = [
        z_ring(0, half(zr, 0), True),
        z_ring(1, half(zr, 1), False),
        z_ring(2, half(zc, 0), True),
        z_ring(3, half(zc, 1), False),
    ]
    zids = z_ring(4, lambda k: ids if k == 0 else zi.at[k], True)
    zids.begin()
    for ch in range(4):
        ys[ch].begin()
        zs[ch].begin()

    drain(wr.at[pl.ds(1, 7)], w_r.at[0])
    rest = fetch(wr.at[pl.ds(1, 7)], wsm.at[pl.ds(1, 7)], m_l.at[7])
    own_table.wait()
    rest.wait()

    line = x * NC + c

    def pick(rel):
        source = ybs[(8 - rel) % 8]
        owner_row = (y + rel) % NY
        for r in (4, 5, 2, 3, 6, 7, 1, 0):
            dx, dc = row[r]
            asked = ((NX - dx) % NX) * NC + dc
            for s in range(2):
                block = wsm[asked, owner_row, line * 2 + s]
                if r == 0:
                    rv[rel * 2 + s] = source[block]
                else:
                    sb[rel, r - 1, s] = source[block]
            if r:
                send(
                    sb.at[rel, r - 1],
                    rv.at[pl.ds((r * 8 + rel) * 2, 2)],
                    x_s.at[0],
                    x_r.at[0],
                    peers[r],
                )

    expert_row = lax.broadcasted_iota(jnp.int32, (16, 256), 0)
    slot_row = lax.broadcasted_iota(jnp.int32, (CAPE, 256), 0).astype(F32)

    def one_row(table, e):
        return jnp.sum(jnp.where(expert_row == e, table, 0.0), 0, keepdims=True)

    def local(j):
        return 1 - c if j == 0 else c

    def prepare(k):
        listed = ids[...] if k == 0 else zi[k]
        hot = jnp.where(
            (listed[0:1] == expert_row) | (listed[1:2] == expert_row), 1.0, 0.0
        )
        rank = dot(hot.astype(BF), before[...])
        place_of = jnp.where(hot > 0.5, rank, -1.0)

        def selector(e):
            return jnp.where(slot_row == one_row(place_of, e), 1.0, 0.0).astype(BF)

        for j in range(2):
            picked = selector(2 * z + local(j))
            sel[j, k] = picked
            cots[j, k * CAPE : (k + 1) * CAPE, :] = dot(picked, zc[k]).astype(BF)
        if k == 0:
            for j in range(2):
                for d in range(NZ):
                    pk[j, d * CAPE : (d + 1) * CAPE, :] = selector(
                        2 * ((z + d) % NZ) + local(j)
                    )

    def arrive_y(k):
        for ch in range(4):
            for slot in (k, 8 - k):
                ys[ch].arrive(slot)
        for slot in (k, 8 - k):
            pick((8 - slot) % 8)

    def arrive_z(k):
        for ch in range(4):
            for slot in (k, 8 - k):
                zs[ch].arrive(slot)
        for slot in (k, 8 - k):
            zids.arrive(slot)

    pick(0)
    arrive_y(1)
    arrive_z(1)
    for copy in later:
        copy.wait()
    for k in range(NZ):
        head = (z + NZ - k) % NZ
        opp[k * HD : (k + 1) * HD, :] = op[pl.ds(pl.multiple_of(head * HD, HD), HD), :]
    for k in (0, 1, 7):
        prepare(k)
    arrive_y(2)
    arrive_z(2)
    for k in (2, 6):
        prepare(k)
    arrive_y(3)
    for ring in ys:
        ring.arrive(4)
    pick(4)
    arrive_z(3)
    for ring in zs + [zids]:
        ring.arrive(4)
    for k in (3, 5, 4):
        prepare(k)
    drain(zr.at[pl.ds(1, 7)], z_s.at[0])
    drain(rv.at[pl.ds(16, 112)], x_r.at[0])

    rings = []

    def attend(ch):
        def block(i, carry):
            b = ch * 4 + i
            pairs = [rv[idx[b * 4 + j]] for j in range(4)]
            keys = jnp.concatenate([p[:HD] for p in pairs], 1)
            values = jnp.concatenate([p[HD:] for p in pairs], 1)
            queries = q[:, pl.ds(pl.multiple_of(b * 128, 128), 128)]
            scores = dot(keys, queries, TN) * (1.0 / math.sqrt(HD))
            weights = jnp.exp(scores - jnp.max(scores, 0, keepdims=True))
            total = jnp.sum(weights, 0, keepdims=True)
            out = dot(values, weights.astype(BF)) / total
            at[0, ch, :, pl.ds(pl.multiple_of(i * 128, 128), 128)] = out.astype(BF)
            return carry

        lax.fori_loop(0, 4, block, 0, unroll=True)
        ring = Ring(
            lambda k: at.at[k, ch],
            lambda k: a_s.at[0],
            lambda k: a_r.at[ch, k - 1],
            up_z, down_z, ch < 2,
        )
        ring.begin()
        rings.append(ring)

    def arrive(k, ch):
        rings[ch].arrive(k)
        if k < 4:
            rings[ch].arrive(8 - k)

    def home(ch):
        mixed = at[:, ch].reshape(256, 512)
        projected = dot(mixed, opp[...], TN)
        for i in range(2):
            k = (z + NZ - (2 * ch + i)) % NZ
            stream = (zr[k].astype(F32) + projected[i * 256 : (i + 1) * 256]).astype(BF)
            wide = stream.astype(F32)
            inv = lax.rsqrt(jnp.mean(wide * wide, -1, keepdims=True) + norm_eps)
            normed = (wide * inv * gain[...]).astype(BF)
            zr[k] = stream
            at_rows = pl.ds(pl.multiple_of(k * CAPE, CAPE), CAPE)
            for j in range(2):
                rows[j, at_rows, :] = dot(sel[j, k], normed).astype(BF)

    attend(0)
    attend(1)
    attend(2)
    arrive(1, 0)
    attend(3)
    for k, ch in (
        (1, 1), (2, 0), (1, 2), (2, 1), (1, 3), (3, 0), (2, 2), (3, 1), (2, 3), (4, 0), (3, 2),
    ):
        arrive(k, ch)
    home(0)
    arrive(4, 1)
    arrive(3, 3)
    home(1)
    arrive(4, 2)
    home(2)
    arrive(4, 3)
    home(3)

    chains = range(2)

    def cross_x(i):
        pair[i].wait_recv()
        own = ga if i == 0 else gb
        t1[i] = (own[1].astype(F32) + rc[i].astype(F32)).astype(BF)
        for d in (2, 1, 3):
            to = (x + d) % NX
            send(
                t1.at[i, pl.ds(pl.multiple_of(to * 128, 128), 128)],
                rx.at[i, d], gx_s.at[i], gx_r.at[i], x_dev[d],
            )

    for j in range(2):
        e = local(j)
        inp, outp = w_in[e], w_out[e]
        x_rows = rows[j]
        logits = dot(x_rows, router[...], NT)
        lane = lax.broadcasted_iota(jnp.int32, (512, 16), 1)
        gate = jax.nn.sigmoid(
            jnp.sum(jnp.where(lane == 2 * z + e, logits, 0.0), 1, keepdims=True)
        )
        cot_rows = cots[j].astype(F32)
        scaled = (gate * cot_rows).astype(BF)
        pre = dot(x_rows, inp)
        grad_hidden = dot(scaled, outp, NT)
        square = pre * pre
        half_up = 0.5 + 0.5 * jnp.tanh(pre * (root_two_pi + root_two_pi * cubic_term * square))
        hidden = (pre * half_up).astype(BF)
        slope = half_up * (
            1.0
            + (1.0 - half_up) * pre * (2.0 * root_two_pi + 6.0 * root_two_pi * cubic_term * square)
        )
        grad_pre = (grad_hidden * slope).astype(BF)

        def weights_part():
            gb[j] = dot(hidden, scaled, TN).astype(BF)
            grad_in = dot(x_rows, grad_pre, TN).astype(BF)
            ga[j, 0:256, :] = grad_in[:, 0:256]
            ga[j, 256:512, :] = grad_in[:, 256:512]

        def rows_part():
            made = dot(hidden, outp)
            grad_rows = dot(grad_pre, inp, NT)
            grad_gate = jnp.sum(cot_rows * made, -1, keepdims=True)
            grad_logit = grad_gate * gate * (1.0 - gate)
            column = one_row(router[...].astype(F32), 2 * z + e)
            first = (gate * made).astype(BF)
            second = (grad_rows + grad_logit * column).astype(BF)
            for k in (4, 3, 5, 2, 6, 1, 7, 0):
                target = ret if k else rr
                target[j, k, :, 0:256] = first[k * CAPE : (k + 1) * CAPE]
                target[j, k, :, 256:512] = second[k * CAPE : (k + 1) * CAPE]
                if k:
                    send(ret.at[j, k], rr.at[j, k], r_s.at[j], r_r.at[j], z_dev[k])

        if j == 0:
            rows_part()
            weights_part()
            pair = [
                send(g.at[0], rc.at[i], c_s.at[i], c_r.at[i], partner)
                for i, g in enumerate((ga, gb))
            ]
        else:
            weights_part()
            for i in chains:
                cross_x(i)
            rows_part()

    for i in chains:
        total = t1[i, pl.ds(pl.multiple_of(x * 128, 128), 128), :].astype(F32)
        drain(rx.at[i, pl.ds(1, 3)], gx_r.at[i])
        for d in range(1, NX):
            total += rx[i, d].astype(F32)
        t2[i] = total.astype(BF)
        for d in (4, 3, 5, 2, 6, 1, 7):
            to = (y + d) % NY
            send(
                t2.at[i, pl.ds(pl.multiple_of(to * 16, 16), 16)],
                ry.at[i, d], gy_s.at[i], gy_r.at[i], y_dev[d],
            )

    def span(size):
        first = {16: x * 128 + y * 16, 128: x * 128, 512: 0}[size] + c * 512
        return pl.ds(pl.multiple_of(first, size), size)

    for i in chains:
        total = t2[i, pl.ds(pl.multiple_of(y * 16, 16), 16), :].astype(F32)
        drain(ry.at[i, pl.ds(1, 7)], gy_r.at[i])
        for d in range(1, NY):
            total += ry[i, d].astype(F32)
        full[i, span(16), :] = total.astype(BF)
        for d in (4, 3, 5, 2, 6, 1, 7):
            part = full.at[i, span(16)]
            send(part, part, hy_s.at[i], hy_r.at[i], y_dev[d])
    for i in chains:
        drain(ry.at[i, pl.ds(1, 7)], hy_r.at[i])
        for d in (2, 1, 3):
            part = full.at[i, span(128)]
            send(part, part, hx_s.at[i], hx_r.at[i], x_dev[d])

    def gathered(j):
        return dot(pk[j], rr[j].reshape(512, 512), TN)

    drain(rr.at[0, pl.ds(1, 7)], r_r.at[0])
    total = gathered(0)
    out_c = []
    for i in chains:
        drain(rx.at[i, pl.ds(1, 3)], hx_r.at[i])
        part = full.at[i, span(512)]
        out_c.append(send(part, part, hc_s.at[i], hc_r.at[i], partner))
    for copy in out_c:
        copy.wait_recv()
    kept = fetch(full, grads, m_l.at[8])

    drain(rr.at[1, pl.ds(1, 7)], r_r.at[1])
    total += gathered(1)
    wide = zr[0].astype(F32)
    inv = lax.rsqrt(jnp.mean(wide * wide, -1, keepdims=True) + norm_eps)
    layer_out[...] = (wide + total[:, 0:256]).astype(BF)
    gained = total[:, 256:512] * gain[...]
    mean = jnp.mean(wide * gained, -1, keepdims=True)
    grad_stream[...] = (
        zc[0].astype(F32) + inv * gained - wide * (inv * inv * inv) * mean
    ).astype(BF)

    kept.wait()
    drain(wr.at[pl.ds(1, 7)], w_s.at[0])
    drain(rv.at[pl.ds(16, 112)], y_s.at[0])
    drain(zc.at[pl.ds(1, 7)], z_s.at[1])
    drain(zi.at[pl.ds(1, 7)], z_s.at[2])
    drain(sb, x_s.at[0])
    drain(at.at[pl.ds(1, 7)], a_s.at[0])
    for copy in pair + out_c:
        copy.wait_send()
    for i in chains:
        drain(ret.at[i, pl.ds(1, 7)], r_s.at[i])
        drain(rx.at[i, pl.ds(1, 3)], gx_s.at[i])
        drain(ry.at[i, pl.ds(1, 7)], gy_s.at[i])
        drain(ry.at[i, pl.ds(1, 7)], hy_s.at[i])
        drain(rx.at[i, pl.ds(1, 3)], hx_s.at[i])


VM = pl.BlockSpec(memory_space=pltpu.VMEM)
SM = pl.BlockSpec(memory_space=pltpu.SMEM)
HB = pl.BlockSpec(memory_space=pltpu.HBM)
DMA = pltpu.SemaphoreType.DMA


def layer(*args):
    def vm(*shape, dtype=BF):
        return pltpu.VMEM(shape, dtype)

    return pl.pallas_call(
        layer_kernel,
        name="layer",
        out_shape=(
            jax.ShapeDtypeStruct((2, 1024, 256), BF),
            jax.ShapeDtypeStruct((256, 256), BF),
            jax.ShapeDtypeStruct((256, 256), BF),
        ),
        in_specs=[SM] + [VM] * 4 + [HB] * 8,
        out_specs=(HB, VM, VM),
        scratch_shapes=[vm(16, 64, 128)] * 8
        + [
            vm(8, 256, 256), vm(8, 256, 256), vm(8, 2, 256, dtype=jnp.int32),
            vm(8, 8, 128, dtype=jnp.int32), pltpu.SMEM((8, 8, 128), jnp.int32),
            vm(8, 7, 2, 64, 128), vm(128, 64, 128), vm(8, 4, 32, 512),
            vm(32, 2048), vm(256, 256), vm(256, 256), vm(2, 256, 512), vm(2, 512, 256),
            vm(256, 256), vm(2, 8, CAPE, 256), vm(2, 512, 256),
            vm(2, 512, 256), vm(2, 512, 256),
            vm(2, 512, 256), vm(2, 512, 256), vm(2, 8, CAPE, 512), vm(2, 8, CAPE, 512),
            vm(2, 512, 256), vm(2, 512, 256), vm(2, 4, 128, 256),
            vm(2, 128, 256), vm(2, 8, 16, 256), vm(2, 1024, 256),
            vm(2, 32, 2048), DMA((2,)), DMA((9,)), DMA((1,)), DMA((4, 7)), DMA((3,)), DMA((5, 7)),
            DMA((1,)), DMA((1,)), DMA((1,)), DMA((1,)), DMA((1,)), DMA((4, 7)),
        ]
        + [DMA((2,))] * 14,
        compiler_params=pltpu.CompilerParams(
            collective_id=0, has_side_effects=True, vmem_limit_bytes=66_000_000
        ),
    )(*args)


def widen_kernel(
    grads, layer_in, grad_in, ga, gb, layer_out, grad_out, held, wide_a, wide_b, rows, i_s, o_s
):
    loads = [
        pltpu.make_async_copy(
            grads.at[i, pl.ds(e * 512, 512)], held.at[i, e], i_s.at[2 * i + e]
        )
        for i in range(2)
        for e in range(2)
    ]
    loads += [
        pltpu.make_async_copy(layer_in, rows.at[0], i_s.at[4]),
        pltpu.make_async_copy(grad_in, rows.at[1], i_s.at[5]),
    ]
    for load in loads:
        load.start()
    stores = []
    for n, load in enumerate(loads):
        load.wait()
        i, e = n // 2, n % 2
        if i == 0:
            wide_a[e, :, 0:256] = held[0, e, 0:256].astype(F32)
            wide_a[e, :, 256:512] = held[0, e, 256:512].astype(F32)
            pair = (wide_a.at[e], ga.at[e])
        elif i == 1:
            wide_b[e] = held[1, e].astype(F32)
            pair = (wide_b.at[e], gb.at[e])
        else:
            pair = (rows.at[e], (layer_out, grad_out)[e])
        store = pltpu.make_async_copy(pair[0], pair[1], o_s.at[n])
        store.start()
        stores.append(store)
    for store in stores:
        store.wait()


def widen(*args):
    return pl.pallas_call(
        widen_kernel,
        name="widen",
        out_shape=(
            jax.ShapeDtypeStruct((2, 256, 512), F32),
            jax.ShapeDtypeStruct((2, 512, 256), F32),
            jax.ShapeDtypeStruct((256, 256), BF),
            jax.ShapeDtypeStruct((256, 256), BF),
        ),
        in_specs=[HB] * 3,
        out_specs=(HB,) * 4,
        scratch_shapes=[
            pltpu.VMEM((2, 2, 512, 256), BF),
            pltpu.VMEM((2, 256, 512), F32),
            pltpu.VMEM((2, 512, 256), F32),
            pltpu.VMEM((2, 256, 256), BF),
            DMA((6,)),
            DMA((6,)),
        ],
        compiler_params=pltpu.CompilerParams(vmem_limit_bytes=66_000_000),
    )(*args)


def tables(block_list):
    y, x, c, _ = place()
    asked = block_list.reshape(-1)
    owner, inner = asked // 16, asked % 16
    entry = jnp.arange(64, dtype=jnp.int32)
    earlier = (owner[:, None] == owner[None, :]) & (entry[None, :] < entry[:, None])
    rank = jnp.sum(earlier.astype(jnp.int32), 1)
    owner_y, line = owner // (NX * NC), owner % (NX * NC)
    rows = jnp.arange(8, dtype=jnp.int32)[:, None, None]
    lanes = jnp.arange(128, dtype=jnp.int32)[None, :, None]
    hit = (owner_y[None, None, :] == rows) & ((line * 2 + rank)[None, None, :] == lanes)
    wanted = jnp.sum(jnp.where(hit, inner[None, None, :], 0), -1)
    supplier = (x - line // NC) % NX * NC + (c - line % NC) % NC
    index = (supplier * 8 + (owner_y - y) % NY) * 2 + rank
    return index, wanted


def shards(
    query_cols, key_cols, value_cols, block_list, residual, out_proj, norm_gain,
    router_weight, expert_ids, expert_in, expert_out, cotangent,
):
    index, wanted = tables(block_list)
    grads, layer_out, grad_stream = layer(
        index, wanted, expert_ids.T, norm_gain.reshape(1, 256), router_weight.T,
        key_cols, value_cols, query_cols, residual, cotangent, out_proj, expert_in, expert_out,
    )
    grad_in, grad_out, layer_out, grad_stream = widen(grads, layer_out, grad_stream)
    return layer_out, grad_stream, grad_in, grad_out


def solution(mesh):
    assert (mesh.shape["seq"], mesh.shape["expert"]) == (NY * NX * NC, NZ)
    return jax.shard_map(
        shards,
        mesh=mesh,
        in_specs=(
            P("expert", "seq"),
            P("expert", "seq"),
            P("expert", "seq"),
            P("seq", None),
            P(("seq", "expert"), None),
            P(),
            P(),
            P(),
            P(("seq", "expert"), None),
            P("expert", None, None),
            P("expert", None, None),
            P(("seq", "expert"), None),
        ),
        out_specs=(
            P(("seq", "expert"), None),
            P(("seq", "expert"), None),
            P("expert", None, None),
            P("expert", None, None),
        ),
        check_vma=False,
    )
```
